32 devices in a mesh: fsdp: 4 (over y, x), rep: 8 (over z, core).
Axes of the slice: x: 2, y: 2, z: 4, core: 2. Of those that a mesh axis runs over, the one named last changes fastest.
Arguments:
- gradient: float32 [11264, 8192], P('fsdp', 'rep'), may hold values from -6 to 6
- row_counts: int32 [4], replicated, may hold values from 1 to 2816, 8192 in all
- owners: int32 [16, 16], P(None, 'rep'), may hold values from 0 to 3, as said below
- refresh_flags: int32 [16, 16], P(None, 'rep'), may hold values 0 or 1
- stat_left: float32 [16, 16, 512, 512], P('fsdp', 'rep'), as said below
- stat_right: float32 [16, 16, 512, 512], P('fsdp', 'rep'), as said below
- root_left: float32 [16, 16, 512, 512], P('fsdp', 'rep'), as said below
- root_right: float32 [16, 16, 512, 512], P('fsdp', 'rep'), as said below
Outputs:
- direction: bfloat16 [11264, 8192], P('fsdp')
- new_left: float32 [16, 16, 512, 512], P('fsdp', 'rep')
- new_right: float32 [16, 16, 512, 512], P('fsdp', 'rep')
The draws below stay inside these ranges and needn't reach their ends.
Inputs may be any that keep to these rules, and one draw needn't show every extreme that they name: `owners`: in each column band of blocks every fsdp index owns exactly 4 blocks. `stat_left`: symmetric positive definite. `stat_right`: symmetric positive definite. `root_left`: symmetric positive definite. `root_right`: symmetric positive definite.
All inputs are finite; a program needn't handle non-finite values. No bound on the sum of `refresh_flags` on one device may be relied on, other than what follows from the above.
Results may differ from the reference program's by a relative error of at most 0.001.
Values may be sent and summed in bfloat16 or wider, within the bound.
A program may use at most 256 MiB of HBM per device.

```python
import math
import jax
import jax.numpy as jnp
import numpy as np
from jax import lax

COLS = 8192
ROWS = 8192
BLOCK = 512
ITERS = 3
CAP = 2816
BANDS = 16
NCB = 16
SLOTS = 4
N_FSDP = 4


def definite(key, low, high):
    shape = (N_FSDP * SLOTS, NCB, BLOCK, BLOCK)
    offdiag = 0.8 / jnp.sqrt(float(BLOCK))
    uniform_noise = jax.random.uniform(jax.random.fold_in(key, 1), shape, jnp.float32, -1.0, 1.0)
    symmetric = 0.5 * (uniform_noise + jnp.swapaxes(uniform_noise, -1, -2))
    log_scales = jax.random.uniform(jax.random.fold_in(key, 2), shape[:-1], jnp.float32, jnp.log(low), jnp.log(high))
    scales = jnp.exp(log_scales)
    core_matrix = jnp.eye(BLOCK, dtype=jnp.float32) + offdiag * symmetric
    return scales[..., :, None] * core_matrix * scales[..., None, :]


def draw_owners(key, part):
    column_keys = jax.random.split(jax.random.fold_in(key, 11), NCB)
    orders = jax.vmap(lambda one_key: jax.random.permutation(one_key, BANDS))(column_keys)
    return (orders.T // SLOTS).astype(jnp.int32)


def draw_stat_left(key, part):
    return BLOCK * definite(jax.random.fold_in(key, 21), 1.0, 3.2)


def draw_stat_right(key, part):
    return BLOCK * definite(jax.random.fold_in(key, 31), 1.0, 3.2)


def draw_root_left(key, part):
    return 0.2 * definite(jax.random.fold_in(key, 41), 1.0, 3.2)


def draw_root_right(key, part):
    return 0.2 * definite(jax.random.fold_in(key, 51), 1.0, 3.2)


def plant(drawn, stream_key, low, largest):
    place = [jax.random.randint(jax.random.fold_in(stream_key, axis), (), 0, length) for axis, length in enumerate(drawn.shape)]
    widest = drawn.shape.index(max(drawn.shape))
    neighbour = place[:widest] + [(place[widest] + 1) % drawn.shape[widest]] + place[widest + 1:]
    return drawn.at[tuple(place)].set(low).at[tuple(neighbour)].set(largest)


def levels(key, dims, cuts, low, largest):
    level, own = 1.0, jax.random.fold_in(key, 6)
    for axis_at, blocks in cuts:
        steps = jnp.exp(jax.random.uniform(jax.random.fold_in(own, axis_at), (blocks,), jnp.float32, low / len(cuts), largest / len(cuts)))
        level = level * jnp.repeat(steps, dims[axis_at] // blocks).reshape([-1 if axis == axis_at else 1 for axis in range(len(dims))])
    return level


def split_up(count, total, bound, skew):
    portions = [(1 << 20) // math.isqrt(standing ** skew) + 1 for standing in range(2, count + 1)]
    surplus, holding = total - bound - (count - 1), [1] * (count - 1)
    while surplus > 0:
        candidates = [i for i in range(count - 1) if holding[i] < bound]
        whole, left = sum([portions[i] for i in candidates]), surplus
        for i in candidates:
            extra = min(bound - holding[i], max(1, left * portions[i] // whole), surplus)
            holding[i] = holding[i] + extra
            surplus = surplus - extra
    return np.array([bound] + holding)


def uneven(key, number_of, total, limit, slope):
    if number_of == 2:
        one = jax.random.randint(key, (), max(1, total - limit), min(limit, total - 1) + 1)
        return jnp.stack([one, total - one])
    lengths = jnp.asarray(split_up(number_of, total, limit, slope), jnp.int32)
    couples = (number_of - 1) // 2
    donor, receiver = lengths[1:1 + 2 * couples:2], lengths[2:2 + 2 * couples:2]
    slack = jnp.minimum(donor - 1, limit - receiver)
    moved = jax.random.randint(jax.random.fold_in(key, 1), (couples,), 0, 1 << 20) % (slack + 1)
    lengths = lengths.at[1:1 + 2 * couples:2].set(donor - moved).at[2:2 + 2 * couples:2].set(receiver + moved)
    return lengths[jax.random.permutation(jax.random.fold_in(key, 2), number_of)]


def scatter_about(rng, shape, scale, bound, pieces=(), kind=jnp.bfloat16):
    drawn = jax.random.normal(rng, shape, jnp.float32) * scale
    if len(pieces) > 0:
        drawn = levels(rng, shape, pieces, -0.22, 0.18) * drawn
    return jnp.clip(drawn, min=-bound, max=bound).astype(kind)


def setup_inputs(seed: int = 0) -> dict:
    streams_of = jax.random.split(jax.random.key(seed), 9)
    return {
        "gradient": scatter_about(streams_of[0], (N_FSDP * CAP, COLS), 1.0, 6.0, ((0, 4), (1, 8)), jnp.float32),
        "row_counts": uneven(streams_of[1], N_FSDP, ROWS, CAP, 2).astype(jnp.int32),
        "owners": draw_owners(jax.random.fold_in(streams_of[8], 71), 0),
        "refresh_flags": plant((jax.random.randint(streams_of[3], (BANDS, NCB), 0, 2) < 1).astype(jnp.int32), jax.random.fold_in(streams_of[3], 1), 0, 1),
        "stat_left": draw_stat_left(jax.random.fold_in(streams_of[8], 71), 0),
        "stat_right": draw_stat_right(jax.random.fold_in(streams_of[8], 71), 0),
        "root_left": draw_root_left(jax.random.fold_in(streams_of[8], 71), 0),
        "root_right": draw_root_right(jax.random.fold_in(streams_of[8], 71), 0),
    }


highest = lax.Precision.HIGHEST
stat_decay = 0.9
graft_eps = 1e-06

def matmul(left_part, right_part):
    return jnp.dot(left_part, right_part, precision=highest, preferred_element_type=jnp.float32)

def inverse_root(matrix, sweeps):
    identity = jnp.eye(matrix.shape[0], dtype=jnp.float32)
    scaling = 2.5 / jnp.sqrt(jnp.sum(matrix * matrix))
    current = identity * jnp.sqrt(jnp.sqrt(scaling))
    moment = matrix * scaling
    for sweep_pos in range(sweeps):
        factor = (5.0 * identity - moment) * 0.25
        current = matmul(current, factor)
        if sweep_pos + 1 < sweeps:
            squared = matmul(factor, factor)
            moment = matmul(matmul(squared, squared), moment)
    return current

def tile_update(grad_tile, left_stat, right_stat, old_left, old_right, refresh_now):
    fresh_left = stat_decay * left_stat + (1.0 - stat_decay) * matmul(grad_tile, grad_tile.T)
    fresh_right = stat_decay * right_stat + (1.0 - stat_decay) * matmul(grad_tile.T, grad_tile)
    left_root, right_root = lax.cond(refresh_now > 0, lambda: (inverse_root(fresh_left, ITERS), inverse_root(fresh_right, ITERS)), lambda: (old_left, old_right))
    precond = matmul(matmul(left_root, grad_tile), right_root)
    graft_ratio = jnp.mean(grad_tile * grad_tile) / (jnp.mean(precond * precond) + graft_eps)
    return (fresh_left, fresh_right, (precond * jnp.sqrt(graft_ratio)).astype(jnp.bfloat16))

def slot_table(owners):
    band_count = owners.shape[0]
    same_owner = owners[:, None, :] == owners[None, :, :]
    ordinal = jnp.arange(band_count, dtype=jnp.int32)
    earlier = (ordinal[None, :] < ordinal[:, None])[:, :, None]
    return lax.optimization_barrier(jnp.sum(jnp.where(same_owner & earlier, 1, 0), axis=1)).astype(jnp.int32)

def reference(gradient, row_counts, owners, refresh_flags, stat_left, stat_right, root_left, root_right):
    tile_size = BLOCK
    offsets = (jnp.cumsum(row_counts) - row_counts).astype(jnp.int32)
    local_rows = jnp.arange(CAP, dtype=jnp.int32)
    live_rows = local_rows[None, :] < row_counts[:, None]
    dest_rows = jnp.where(live_rows, offsets[:, None] + local_rows[None, :], ROWS).reshape(-1).astype(jnp.int32)
    dense_grad = jnp.zeros((ROWS, COLS), gradient.dtype).at[dest_rows].set(gradient, mode='drop')
    slot_rank = slot_table(owners)
    holder = (owners * SLOTS + slot_rank).astype(jnp.int32)

    def update_tile(tile_index):
        band_pos = tile_index // NCB
        column_pos = tile_index % NCB
        grad_tile = lax.dynamic_slice(dense_grad, (band_pos * tile_size, column_pos * tile_size), (tile_size, tile_size))
        state_index = holder[band_pos, column_pos]
        return tile_update(grad_tile, stat_left[state_index, column_pos], stat_right[state_index, column_pos], root_left[state_index, column_pos], root_right[state_index, column_pos], refresh_flags[band_pos, column_pos])
    fresh_lefts, fresh_rights, tile_stack = lax.map(update_tile, jnp.arange(BANDS * NCB, dtype=jnp.int32))
    flat_holder = holder.reshape(-1)
    flat_column = jnp.tile(jnp.arange(NCB, dtype=jnp.int32), BANDS)
    new_left = stat_left.at[flat_holder, flat_column].set(fresh_lefts)
    new_right = stat_right.at[flat_holder, flat_column].set(fresh_rights)
    dense_direction = tile_stack.reshape(BANDS, NCB, tile_size, tile_size).transpose(0, 2, 1, 3).reshape(ROWS, COLS)
    source_rows = jnp.clip(offsets[:, None] + local_rows[None, :], 0, ROWS - 1).reshape(-1)
    picked = dense_direction[source_rows]
    direction = jnp.where(live_rows.reshape(-1)[:, None], picked, jnp.zeros_like(picked))
    return (direction, new_left, new_right)
```

```python
import functools

import jax
import jax.numpy as jnp
from jax import lax
from jax.experimental import pallas as pl
from jax.experimental.pallas import tpu as pltpu
from jax.sharding import PartitionSpec as P

ITERS = 3


stat_decay = 0.9
graft_eps = 1e-06
NN = (((1,), (0,)), ((), ()))
NT = (((1,), (1,)), ((), ()))
TN = (((0,), (0,)), ((), ()))


def split(value):
    high = value.astype(jnp.bfloat16)
    return high, (value - high.astype(jnp.float32)).astype(jnp.bfloat16)


def product(left, right, dims=NN):
    dot = functools.partial(
        lax.dot_general, dimension_numbers=dims, preferred_element_type=jnp.float32
    )
    return dot(left[0], right[0]) + (dot(left[0], right[1]) + dot(left[1], right[0]))


def total(value):
    return jnp.sum(jnp.sum(value, axis=0, keepdims=True), axis=1, keepdims=True)


def update_kernel(
    flags, grad, stat_left, stat_right, root_left, root_right, _left, _right,
    new_left, new_right, tile, roots, moment, factor, *, first,
):
    size = grad.shape[-1]
    grad_value = grad[0]
    parts = split(grad_value)
    fresh_left = stat_decay * stat_left[0, 0] + (1.0 - stat_decay) * product(parts, parts, NT)
    new_left[0, 0] = fresh_left
    fresh_right = stat_decay * stat_right[0, 0] + (1.0 - stat_decay) * product(parts, parts, TN)
    new_right[0, 0] = fresh_right
    refresh = flags[first + pl.program_id(0)] > 0

    @pl.when(refresh)
    def _():
        rows = lax.broadcasted_iota(jnp.int32, (size, size), 0)
        columns = lax.broadcasted_iota(jnp.int32, (size, size), 1)
        diagonal = jnp.where(rows == columns, 1.25, 0.0)
        roots[0] = new_left[0, 0]
        roots[1] = new_right[0, 0]

        @pl.loop(0, 2)
        def _(side):
            matrix = roots[side]
            scaling = 2.5 / jnp.sqrt(total(matrix * matrix))
            scaled = matrix * scaling
            moment[...] = scaled
            first_factor = diagonal - 0.25 * scaled
            factor[...] = first_factor
            roots[side] = first_factor * jnp.sqrt(jnp.sqrt(scaling))

            @pl.loop(0, ITERS - 1)
            def _(sweep):
                parts = split(factor[...])
                squared = split(product(parts, parts))
                fourth = split(product(squared, squared))
                latest = product(fourth, split(moment[...]))
                moment[...] = latest
                following = diagonal - 0.25 * latest
                factor[...] = following
                roots[side] = product(split(roots[side]), split(following))

    @pl.when(jnp.logical_not(refresh))
    def _():
        roots[0] = root_left[0, 0]
        roots[1] = root_right[0, 0]

    grad_again = grad[0]
    half = product(split(roots[0]), split(grad_again))
    precond = product(split(half), split(roots[1]))
    grad_mean = total(grad_again * grad_again) / (size * size)
    precond_mean = total(precond * precond) / (size * size)
    tile[0] = (precond * jnp.sqrt(grad_mean / (precond_mean + graft_eps))).astype(jnp.bfloat16)


def update_blocks(flags, grads, stats, roots, fresh, column, first, length):
    size = grads.shape[-1]

    def state(index, flags):
        return (first + index, column, 0, 0)

    block = pl.BlockSpec((1, 1, size, size), state)
    aliased = fresh is not None
    base = fresh if aliased else ()

    def kernel(*refs):
        if aliased:
            update_kernel(*refs, first=first)
        else:
            update_kernel(*refs[:6], None, None, *refs[6:], first=first)

    flops = 60 * length * 2 * size**3
    moved = length * size * size * 30
    return pl.pallas_call(
        kernel,
        grid_spec=pltpu.PrefetchScalarGridSpec(
            num_scalar_prefetch=1,
            grid=(length,),
            in_specs=[pl.BlockSpec((1, size, size), lambda index, flags: (first + index, 0, 0))]
            + [block] * 4
            + [pl.BlockSpec(memory_space=pl.ANY)] * len(base),
            out_specs=[block, block, pl.BlockSpec((1, size, size), lambda index, flags: (index, 0, 0))],
            scratch_shapes=[
                pltpu.VMEM((2, size, size), jnp.float32),
                pltpu.VMEM((size, size), jnp.float32),
                pltpu.VMEM((size, size), jnp.float32),
            ],
        ),
        out_shape=[
            jax.ShapeDtypeStruct(stats[0].shape, jnp.float32),
            jax.ShapeDtypeStruct(stats[1].shape, jnp.float32),
            jax.ShapeDtypeStruct((length, size, size), jnp.bfloat16),
        ],
        input_output_aliases={6: 0, 7: 1} if aliased else {},
        compiler_params=pltpu.CompilerParams(vmem_limit_bytes=48 << 20),
        cost_estimate=pl.CostEstimate(flops=flops, bytes_accessed=moved, transcendentals=0),
    )(flags, grads, *stats, *roots, *base)


def slot_table(owners):
    band_count = owners.shape[0]
    same_owner = owners[:, None, :] == owners[None, :, :]
    ordinal = jnp.arange(band_count, dtype=jnp.int32)
    earlier = (ordinal[None, :] < ordinal[:, None])[:, :, None]
    return jnp.sum(jnp.where(same_owner & earlier, 1, 0), axis=1).astype(jnp.int32)


def pick(stack, index):
    return lax.dynamic_index_in_dim(stack, index, 0, keepdims=False)


def send_each(choose, me, count):
    pieces = [choose(me)]
    for shift in range(1, count):
        pairs = [(source, (source + shift) % count) for source in range(count)]
        pieces.append(lax.ppermute(choose(lax.rem(me + shift, count)), "fsdp", pairs))
    return pieces


def per_device(
    gradient, row_counts, owners, refresh_flags, stat_left, stat_right, root_left, root_right, *, count
):
    tile_size = stat_left.shape[-1]
    me = lax.axis_index("fsdp")
    capacity, slab_width = gradient.shape
    band_count, columns = owners.shape
    slot_count = stat_left.shape[0]
    part = tile_size // count
    share = -(-capacity // count)
    total_rows = band_count * tile_size
    offsets = (jnp.cumsum(row_counts) - row_counts).astype(jnp.int32)
    slot_rank = slot_table(owners)
    holder = owners * slot_count + slot_rank
    band_ids = jnp.arange(band_count, dtype=jnp.int32)
    column_ids = jnp.arange(columns, dtype=jnp.int32)
    band_at = jnp.sum(
        jnp.where(holder[None, :, :] == band_ids[:, None, None], band_ids[None, :, None], 0), axis=1
    )
    my_bands = lax.dynamic_slice_in_dim(band_at, me * slot_count, slot_count, 0)
    refresh_now = refresh_flags[my_bands, column_ids[None, :]]

    class_rows = jnp.arange(total_rows // count, dtype=jnp.int32)
    row_ids = class_rows * count + me
    source = jnp.sum((offsets[None, :] <= row_ids[:, None]).astype(jnp.int32), axis=-1) - 1
    first_class = (offsets + (me - offsets) % count - me) // count
    arrived_at = ((me - source) % count) * share + class_rows - first_class[source]

    local_rows = jnp.arange(capacity, dtype=jnp.int32)
    global_rows = offsets[me] + local_rows
    live_rows = local_rows < row_counts[me]
    band_pos = jnp.clip(global_rows // tile_size, 0, band_count - 1)
    within = global_rows % tile_size

    cuts = [gradient[:, at * tile_size : (at + 1) * tile_size] for at in range(columns)]

    def scatter(column):
        cut = jnp.pad(cuts[column], ((0, share * count - capacity), (0, 0)))
        classes = cut.reshape(share, count, tile_size).transpose(1, 0, 2)
        return send_each(lambda to: pick(classes, (to - offsets[me]) % count), me, count)

    def relay(column, pieces):
        order = band_at[:, column][:, None] * part + jnp.arange(part, dtype=jnp.int32)
        arrived = jnp.concatenate(pieces, axis=0)
        relayed = arrived.at[arrived_at[order.reshape(-1)]].get(mode="promise_in_bounds")
        relayed = relayed.reshape(count, slot_count * part, tile_size)
        return send_each(lambda to: pick(relayed, to), me, count)

    def assemble(pieces):
        back = (me - jnp.arange(count, dtype=jnp.int32)) % count
        owned = jnp.stack([pick(jnp.stack(pieces), back[at]) for at in range(count)])
        owned = owned.reshape(count, slot_count, part, tile_size).transpose(1, 2, 0, 3)
        return owned.reshape(slot_count, tile_size, tile_size)

    def spread(tiles):
        return send_each(lambda to: tiles, me, count)

    def slab(column, pieces):
        gathered = jnp.concatenate(pieces, axis=0).reshape(-1, tile_size)
        state = holder[band_pos, column]
        owner = state // slot_count
        rank = state % slot_count
        position = (((me - owner) % count) * slot_count + rank) * tile_size + within
        picked = gathered.at[position].get(mode="promise_in_bounds")
        return jnp.where(live_rows[:, None], picked, jnp.zeros_like(picked))

    def run(column, grads, half, fresh):
        cut = max(1, slot_count // 2)
        first, length = ((0, cut), (cut, slot_count - cut))[half]
        if length == 0:
            return fresh, None
        left, right, tiles = update_blocks(
            refresh_now[:, column], grads, (stat_left, stat_right), (root_left, root_right),
            fresh, column, first, length,
        )
        return (left, right), tiles

    def joined(first_half, second_half):
        return first_half if second_half is None else jnp.concatenate([first_half, second_half])

    barrier = lax.optimization_barrier
    fresh = None
    grads = assemble(relay(0, scatter(0)))
    waiting, slabs = None, []
    for column in range(columns):
        more = column + 1 < columns
        if more:
            cuts[column + 1], grads = barrier((cuts[column + 1], grads))
            pieces = scatter(column + 1)
        fresh, low = run(column, grads, 0, fresh)
        if waiting is not None:
            waiting, fresh, low = barrier((waiting, fresh, low))
            slabs.append(slab(column - 1, waiting))
            slabs[-1], grads = barrier((slabs[-1], grads))
        if more:
            pieces, fresh, low = barrier((pieces, fresh, low))
            pieces = relay(column + 1, pieces)
        fresh, high = run(column, grads, 1, fresh)
        if more:
            pieces, fresh, high = barrier((pieces, fresh, high))
            grads = assemble(pieces)
        waiting = spread(joined(low, high))
    slabs.append(slab(columns - 1, waiting))
    gathered = [lax.all_gather(rows, "rep", axis=0, tiled=False) for rows in slabs]
    direction = jnp.zeros((capacity, gathered[0].shape[0] * columns * tile_size), jnp.bfloat16)
    for column, wide in enumerate(gathered):
        for at in range(wide.shape[0]):
            start = (at * columns + column) * tile_size
            direction = lax.dynamic_update_slice(direction, wide[at], (0, start))
    new_left, new_right = fresh
    return (direction, new_left, new_right)


def solution(mesh):
    count = mesh.shape["fsdp"]

    def body(*arrays):
        return per_device(*arrays, count=count)

    return jax.shard_map(
        body,
        mesh=mesh,
        in_specs=(
            P("fsdp", "rep"),
            P(),
            P(None, "rep"),
            P(None, "rep"),
            P("fsdp", "rep", None, None),
            P("fsdp", "rep", None, None),
            P("fsdp", "rep", None, None),
            P("fsdp", "rep", None, None),
        ),
        out_specs=(P("fsdp", None), P("fsdp", "rep", None, None), P("fsdp", "rep", None, None)),
        check_vma=False,
    )
```

```python
import functools

import jax
import jax.numpy as jnp
from jax import lax
from jax.experimental import pallas as pl
from jax.experimental.pallas import tpu as pltpu
from jax.sharding import PartitionSpec as P

ITERS = 3
LANES = 128


stat_decay = 0.9
graft_eps = 1e-06
NN = (((1,), (0,)), ((), ()))
NT = (((1,), (1,)), ((), ()))
TN = (((0,), (0,)), ((), ()))


def split(value):
    high = value.astype(jnp.bfloat16)
    return high, (value - high.astype(jnp.float32)).astype(jnp.bfloat16)


def product(left, right, dims=NN):
    dot = functools.partial(
        lax.dot_general, dimension_numbers=dims, preferred_element_type=jnp.float32
    )
    return dot(left[0], right[0]) + (dot(left[0], right[1]) + dot(left[1], right[0]))


def total(value):
    return jnp.sum(jnp.sum(value, axis=0, keepdims=True), axis=1, keepdims=True)


def update_kernel(
    flags, grad, stat_left, stat_right, root_left, root_right, _left, _right,
    new_left, new_right, tile, roots, moment, factor, whole, *, first,
):
    size = grad.shape[-1]
    count = grad.shape[0]
    for residue in range(count):
        piece = grad[residue, 0]
        for at in range(size // LANES):
            lanes = piece[:, at * LANES : (at + 1) * LANES]
            whole[at, pl.ds(residue, size // count, stride=count), :] = lanes
    grad_value = jnp.concatenate([whole[at] for at in range(size // LANES)], axis=1)
    parts = split(grad_value)
    fresh_left = stat_decay * stat_left[0, 0] + (1.0 - stat_decay) * product(parts, parts, NT)
    new_left[0, 0] = fresh_left
    fresh_right = stat_decay * stat_right[0, 0] + (1.0 - stat_decay) * product(parts, parts, TN)
    new_right[0, 0] = fresh_right
    refresh = flags[first + pl.program_id(0)] > 0

    @pl.when(refresh)
    def _():
        rows = lax.broadcasted_iota(jnp.int32, (size, size), 0)
        columns = lax.broadcasted_iota(jnp.int32, (size, size), 1)
        diagonal = jnp.where(rows == columns, 1.25, 0.0)
        roots[0] = new_left[0, 0]
        roots[1] = new_right[0, 0]

        @pl.loop(0, 2)
        def _(side):
            matrix = roots[side]
            scaling = 2.5 / jnp.sqrt(total(matrix * matrix))
            scaled = matrix * scaling
            moment[...] = scaled
            first_factor = diagonal - 0.25 * scaled
            factor[...] = first_factor
            roots[side] = first_factor * jnp.sqrt(jnp.sqrt(scaling))

            @pl.loop(0, ITERS - 1)
            def _(sweep):
                parts = split(factor[...])
                squared = split(product(parts, parts))
                fourth = split(product(squared, squared))
                latest = product(fourth, split(moment[...]))
                moment[...] = latest
                following = diagonal - 0.25 * latest
                factor[...] = following
                roots[side] = product(split(roots[side]), split(following))

    @pl.when(jnp.logical_not(refresh))
    def _():
        roots[0] = root_left[0, 0]
        roots[1] = root_right[0, 0]

    grad_again = jnp.concatenate([whole[at] for at in range(size // LANES)], axis=1)
    half = product(split(roots[0]), split(grad_again))
    precond = product(split(half), split(roots[1]))
    grad_mean = total(grad_again * grad_again) / (size * size)
    precond_mean = total(precond * precond) / (size * size)
    tile[0] = (precond * jnp.sqrt(grad_mean / (precond_mean + graft_eps))).astype(jnp.bfloat16)


def update_blocks(flags, grads, stats, roots, fresh, column, first, length):
    size = grads.shape[-1]
    count = grads.shape[0]

    def state(index, flags):
        return (first + index, column, 0, 0)

    block = pl.BlockSpec((1, 1, size, size), state)
    aliased = fresh is not None
    base = fresh if aliased else ()

    def kernel(*refs):
        if aliased:
            update_kernel(*refs, first=first)
        else:
            update_kernel(*refs[:6], None, None, *refs[6:], first=first)

    flops = 60 * length * 2 * size**3
    moved = length * size * size * 30
    return pl.pallas_call(
        kernel,
        grid_spec=pltpu.PrefetchScalarGridSpec(
            num_scalar_prefetch=1,
            grid=(length,),
            in_specs=[pl.BlockSpec((count, 1, size // count, size), lambda index, flags: (0, first + index, 0, 0))]
            + [block] * 4
            + [pl.BlockSpec(memory_space=pl.ANY)] * len(base),
            out_specs=[block, block, pl.BlockSpec((1, size, size), lambda index, flags: (index, 0, 0))],
            scratch_shapes=[
                pltpu.VMEM((2, size, size), jnp.float32),
                pltpu.VMEM((size, size), jnp.float32),
                pltpu.VMEM((size, size), jnp.float32),
                pltpu.VMEM((size // LANES, size, LANES), jnp.float32),
            ],
        ),
        out_shape=[
            jax.ShapeDtypeStruct(stats[0].shape, jnp.float32),
            jax.ShapeDtypeStruct(stats[1].shape, jnp.float32),
            jax.ShapeDtypeStruct((length, size, size), jnp.bfloat16),
        ],
        input_output_aliases={6: 0, 7: 1} if aliased else {},
        compiler_params=pltpu.CompilerParams(vmem_limit_bytes=48 << 20),
        cost_estimate=pl.CostEstimate(flops=flops, bytes_accessed=moved, transcendentals=0),
    )(flags, grads, *stats, *roots, *base)


def deal_kernel(rows, classes):
    count, length = classes.shape[:2]
    for residue in range(count):
        classes[residue] = rows[pl.ds(residue, length, stride=count), :]


def deal(gradient, token, column, size, count):
    share = gradient.shape[0] // count
    steps = 2 if share % 16 == 0 else 1
    lanes = size // LANES
    length = share // steps

    def kernel(rows, _token, classes):
        deal_kernel(rows, classes)

    return pl.pallas_call(
        kernel,
        grid=(steps, lanes),
        in_specs=[
            pl.BlockSpec((length * count, LANES), lambda step, lane: (step, column * lanes + lane)),
            pl.BlockSpec(memory_space=pl.ANY),
        ],
        out_specs=pl.BlockSpec((count, length, LANES), lambda step, lane: (0, step, lane)),
        out_shape=jax.ShapeDtypeStruct((count, share, size), gradient.dtype),
        cost_estimate=pl.CostEstimate(
            flops=0, bytes_accessed=8 * share * count * size, transcendentals=0
        ),
    )(gradient, token)


def lookup(table, index):
    result = jnp.zeros(index.shape, table.dtype)
    for at in range(table.shape[0]):
        result = result + jnp.where(index == at, table[at], 0)
    return result


def slot_table(owners):
    band_count = owners.shape[0]
    same_owner = owners[:, None, :] == owners[None, :, :]
    ordinal = jnp.arange(band_count, dtype=jnp.int32)
    earlier = (ordinal[None, :] < ordinal[:, None])[:, :, None]
    return jnp.sum(jnp.where(same_owner & earlier, 1, 0), axis=1).astype(jnp.int32)


def pick(stack, index):
    return lax.dynamic_index_in_dim(stack, index, 0, keepdims=False)


def send_each(choose, me, count):
    pieces = [choose(me)]
    for shift in range(1, count):
        pairs = [(source, (source + shift) % count) for source in range(count)]
        pieces.append(lax.ppermute(choose(lax.rem(me + shift, count)), "fsdp", pairs))
    return pieces


def per_device(
    gradient, row_counts, owners, refresh_flags, stat_left, stat_right, root_left, root_right, *, count
):
    tile_size = stat_left.shape[-1]
    me = lax.axis_index("fsdp")
    capacity, slab_width = gradient.shape
    band_count, columns = owners.shape
    slot_count = stat_left.shape[0]
    part = tile_size // count
    share = capacity // count
    total_rows = band_count * tile_size
    offsets = (jnp.cumsum(row_counts) - row_counts).astype(jnp.int32)
    slot_rank = slot_table(owners)
    holder = owners * slot_count + slot_rank
    band_ids = jnp.arange(band_count, dtype=jnp.int32)
    column_ids = jnp.arange(columns, dtype=jnp.int32)
    band_at = jnp.sum(
        jnp.where(holder[None, :, :] == band_ids[:, None, None], band_ids[None, :, None], 0), axis=1
    )
    my_bands = lax.dynamic_slice_in_dim(band_at, me * slot_count, slot_count, 0)
    refresh_now = refresh_flags[my_bands, column_ids[None, :]]

    first_class = (offsets + (me - offsets) % count - me) // count

    def arrival(class_rows):
        row_ids = class_rows * count + me
        source = jnp.sum((offsets[:, None] <= row_ids[None, :]).astype(jnp.int32), axis=0) - 1
        return ((me - source) % count) * share + class_rows - lookup(first_class, source)

    local_rows = jnp.arange(capacity, dtype=jnp.int32)
    global_rows = offsets[me] + local_rows
    live_rows = local_rows < row_counts[me]
    band_pos = jnp.clip(global_rows // tile_size, 0, band_count - 1)
    within = global_rows % tile_size

    def scatter(column, token):
        classes = deal(gradient, token, column, tile_size, count)
        return send_each(lambda to: pick(classes, (to - offsets[me]) % count), me, count)

    def relay(column, pieces):
        order = band_at[:, column][:, None] * part + jnp.arange(part, dtype=jnp.int32)
        order = order.reshape(-1)
        arrived = jnp.concatenate(pieces, axis=0)
        relayed = arrived.at[arrival(order)].get(mode="promise_in_bounds")
        relayed = relayed.reshape(count, slot_count * part, tile_size)
        return send_each(lambda to: pick(relayed, to), me, count)

    def assemble(pieces):
        stacked = jnp.stack(pieces)
        ordered = jnp.stack([pick(stacked, (me - at) % count) for at in range(count)])
        return ordered.reshape(count, slot_count, part, tile_size)

    def spread(tiles):
        return send_each(lambda to: tiles, me, count)

    def slab(column, pieces):
        gathered = jnp.concatenate(pieces, axis=0).reshape(-1, tile_size)
        state = lookup(holder[:, column], band_pos)
        owner = state // slot_count
        rank = state % slot_count
        position = (((me - owner) % count) * slot_count + rank) * tile_size + within
        picked = gathered.at[position].get(mode="promise_in_bounds")
        return jnp.where(live_rows[:, None], picked, jnp.zeros_like(picked))

    def run(column, grads, half, fresh):
        cut = max(1, slot_count // 2)
        first, length = ((0, cut), (cut, slot_count - cut))[half]
        if length == 0:
            return fresh, None
        left, right, tiles = update_blocks(
            refresh_now[:, column], grads, (stat_left, stat_right), (root_left, root_right),
            fresh, column, first, length,
        )
        return (left, right), tiles

    def joined(first_half, second_half):
        return first_half if second_half is None else jnp.concatenate([first_half, second_half])

    barrier = lax.optimization_barrier
    fresh = None
    grads = assemble(relay(0, scatter(0, row_counts)))
    waiting, slabs = None, []
    for column in range(columns):
        more = column + 1 < columns
        if more:
            pieces = scatter(column + 1, grads)
        fresh, low = run(column, grads, 0, fresh)
        if waiting is not None:
            waiting, fresh, low = barrier((waiting, fresh, low))
            slabs.append(slab(column - 1, waiting))
            slabs[-1], grads = barrier((slabs[-1], grads))
        if more:
            pieces, fresh, low = barrier((pieces, fresh, low))
            pieces = relay(column + 1, pieces)
        fresh, high = run(column, grads, 1, fresh)
        if more:
            pieces, fresh, high = barrier((pieces, fresh, high))
            grads = assemble(pieces)
        waiting = spread(joined(low, high))
    slabs.append(slab(columns - 1, waiting))
    gathered = [lax.all_gather(rows, "rep", axis=0, tiled=False) for rows in slabs]
    direction = jnp.zeros((capacity, gathered[0].shape[0] * columns * tile_size), jnp.bfloat16)
    for column, wide in enumerate(gathered):
        for at in range(wide.shape[0]):
            start = (at * columns + column) * tile_size
            direction = lax.dynamic_update_slice(direction, wide[at], (0, start))
    new_left, new_right = fresh
    return (direction, new_left, new_right)


def solution(mesh):
    count = mesh.shape["fsdp"]

    def body(*arrays):
        return per_device(*arrays, count=count)

    return jax.shard_map(
        body,
        mesh=mesh,
        in_specs=(
            P("fsdp", "rep"),
            P(),
            P(None, "rep"),
            P(None, "rep"),
            P("fsdp", "rep", None, None),
            P("fsdp", "rep", None, None),
            P("fsdp", "rep", None, None),
            P("fsdp", "rep", None, None),
        ),
        out_specs=(P("fsdp", None), P("fsdp", "rep", None, None), P("fsdp", "rep", None, None)),
        check_vma=False,
    )
```
